32 devices in a mesh: pb: 8 (over y, x, core), row: 4 (over z).
Axes of the slice: x: 2, y: 2, z: 4, core: 2. Of those that a mesh axis runs over, the one named last changes fastest.
Arguments:
- screened: bfloat16 [16, 2, 1024, 1024], P('pb', None, 'row'), may hold values from -1.0546875 to 1.0546875
- response: bfloat16 [16, 2, 1024, 1024], P(None, None, 'pb', 'row'), may hold values from -0.1875 to 0.1875
- q_owner: int32 [16], replicated, may hold values from 0 to 15, each once
- g_index: int32 [16, 1024], P('pb'), may hold values from 0 to 1023, each once within a row
Outputs:
- tangent: float32 [16, 2, 1024, 1024], P(None, None, ('row', 'pb'))
The draws below stay inside these ranges and needn't reach their ends.
Inputs may be any that keep to these rules, and one draw needn't show every extreme that they name: `q_owner`: each owner slot appears once. `g_index`: each row is a permutation of the 1024 plane waves.
All inputs are finite; a program needn't handle non-finite values.
Results may differ from the reference program's by a relative error of at most 0.0029.
Values may be sent and summed in bfloat16 or wider, within the bound.
A program may use at most 64 MiB of HBM per device.

```python
import jax
import jax.numpy as jnp
from jax import lax

NG = 1024
Q = 16


def shard_levels(stream_key, shape, split, low, high):
    loudness = 1.0
    for axis_at, parts in split:
        heights = jax.random.uniform(jax.random.fold_in(jax.random.fold_in(stream_key, 6), axis_at), (parts,), jnp.float32, low / len(split), high / len(split))
        loudness = loudness * jnp.repeat(jnp.exp(heights), shape[axis_at] // parts).reshape((-1,) + (1,) * (len(shape) - 1 - axis_at))
    return loudness


def normal_values(own_key, shape, scale, reach, shards=(), kind=jnp.bfloat16):
    drawn = scale * jax.random.normal(own_key, shape, jnp.float32)
    if shards:
        drawn = drawn * shard_levels(own_key, shape, shards, -0.22, 0.18)
    return jnp.clip(drawn, -reach, reach).astype(kind)


def setup_inputs(seed: int = 0) -> dict:
    key_list = jax.random.split(jax.random.key(seed), 5)
    return {
        "screened": normal_values(key_list[0], (Q, 2, NG, NG), (NG ** -0.25), 1.0546875, ((0, 8), (2, 4))),
        "response": normal_values(key_list[1], (Q, 2, NG, NG), NG ** -0.5, 0.1875, ((2, 8), (3, 4))),
        "q_owner": jax.random.permutation(key_list[2], Q).astype(jnp.int32),
        "g_index": jax.vmap(lambda own: jax.random.permutation(own, NG))(jax.random.split(key_list[3], Q)).reshape((Q, NG)).astype(jnp.int32),
    }


def complex_product(left, right):
    real_part = jnp.dot(left[0], right[0], preferred_element_type=jnp.float32) - jnp.dot(left[1], right[1], preferred_element_type=jnp.float32)
    imag_part = jnp.dot(left[0], right[1], preferred_element_type=jnp.float32) + jnp.dot(left[1], right[0], preferred_element_type=jnp.float32)
    return jnp.stack((real_part, imag_part), axis=0)


def reference(screened, response, q_owner, g_index):
    inverse = jnp.zeros((Q,), jnp.int32).at[q_owner].set(jnp.arange(Q, dtype=jnp.int32))

    def one_slot(slot):
        source = inverse[slot]
        chi = response[source][:, g_index[slot], :]
        weight = screened[slot]
        halfway = complex_product(weight, chi).astype(jnp.bfloat16)
        return complex_product(halfway, weight)

    per_slot = lax.map(one_slot, jnp.arange(Q, dtype=jnp.int32))
    return jnp.take(per_slot, q_owner, axis=0)
```

```python
import functools

import jax
import jax.numpy as jnp
from jax import lax
from jax.experimental import pallas as pl
from jax.experimental.pallas import tpu as pltpu
from jax.sharding import PartitionSpec as P

F32 = jnp.float32
BF16 = jnp.bfloat16


def to_slots(order, source, target):
    target[...] = source[...]


def from_slots(order, source, target):
    target[...] = source[...].astype(target.dtype)


def team_kernel(
    pb, rows, team, tile,
    response, screened, table, out,
    raw, weight, chi, owner_table, half, half_out, stage,
    chi_sent, chi_got, w_sent, w_got, f_sent, f_got, g_sent, g_got, h_sent, h_got, o_sent, o_got,
):
    slots = response.shape[0]
    per_pb = screened.shape[0]
    size = screened.shape[3]
    groups = pb // team
    block_rows, block_cols = response.shape[2], response.shape[3]
    own_cols = size // team
    w_rows = size // rows
    w_part = w_rows // team
    spread = rows // team
    dests = pb // team
    out_rows = out.shape[2]
    near = rows // 2

    p, r = lax.axis_index("pb"), lax.axis_index("row")
    t, group = p % team, p // team
    slot = group * rows + r

    def same(a, b):
        return jnp.logical_and(a == p, b == r)

    barrier = pltpu.get_barrier_semaphore()

    def greet(k, carry):
        @pl.when(k != p * rows + r)
        def _():
            pl.semaphore_signal(barrier, inc=1, device_id=(k // rows, k % rows), device_id_type=pl.DeviceIdType.MESH)
        return carry

    lax.fori_loop(0, pb * rows, greet, 0)
    pl.semaphore_wait(barrier, pb * rows - 1)

    def send(src, dst, sent, got, at_p, at_r):
        @pl.when(same(at_p, at_r))
        def _():
            pltpu.make_async_copy(src, dst, got).start()

        @pl.when(jnp.logical_not(same(at_p, at_r)))
        def _():
            remote(src, dst, sent, got, at_p, at_r).start()

    def remote(src, dst, sent, got, at_p, at_r):
        return pltpu.make_async_remote_copy(
            src_ref=src, dst_ref=dst, send_sem=sent, recv_sem=got,
            device_id=(at_p, at_r), device_id_type=pl.DeviceIdType.MESH,
        )

    def arrived(ref, sem):
        pltpu.make_async_copy(ref, ref, sem).wait()

    def left(ref, sem, at_p, at_r):
        @pl.when(jnp.logical_not(same(at_p, at_r)))
        def _():
            pltpu.make_async_copy(ref, ref, sem).wait()

    def far_first(k):
        side = r // near
        across = (1 - side) * near + (r + k) % near
        beside = side * near + (r + 1 + k) % near
        return jnp.where(k < near, across, beside)

    holder = r // per_pb
    mine = table.at[r % per_pb]

    @pl.when(t == holder)
    def _():
        pltpu.make_async_copy(mine, owner_table, g_got).start()
        for step in range(1, team):
            remote(mine, owner_table, g_sent.at[step - 1], g_got, group * team + (t + step) % team, r).start()

    member = r // spread

    def chi_place(k):
        at_r = far_first(k // groups)
        at_group = (group + k) % groups
        return at_group * rows + at_r, at_group * team + member, at_r

    def chi_target(from_p, from_r):
        return raw.at[
            :,
            pl.ds(pl.multiple_of(from_p * block_rows, block_rows), block_rows),
            pl.ds(pl.multiple_of((from_r % spread) * block_cols, block_cols), block_cols),
        ]

    def chi_send(k, carry):
        number, at_p, at_r = chi_place(k)
        send(response.at[number], chi_target(p, r), chi_sent.at[k], chi_got.at[p * spread + r % spread], at_p, at_r)
        return carry

    lax.fori_loop(0, slots, chi_send, 0)

    def w_target(block, part):
        start = pl.multiple_of(block * w_rows + part * w_part, w_part)
        return weight.at[:, pl.ds(start, w_part), :]

    def w_place(k):
        i, part = k // team, k % team
        return i, part, group * team + part, t * per_pb + i

    def w_send(k, carry):
        i, part, at_p, at_r = w_place(k)
        src = screened.at[i, :, pl.ds(pl.multiple_of(part * w_part, w_part), w_part), :]
        send(src, w_target(r, part), w_sent.at[k], w_got.at[r], at_p, at_r)
        return carry

    lax.fori_loop(0, per_pb * team, w_send, 0)

    arrived(owner_table, g_got)

    def chi_wait(k, carry):
        arrived(chi_target(k // spread, k % spread), chi_got.at[k])
        return carry

    lax.fori_loop(0, pb * spread, chi_wait, 0)

    def reorder(k, carry):
        start = pl.multiple_of(k * tile, tile)
        wanted = owner_table[:, pl.ds(start, tile)]
        chosen = (lax.broadcasted_iota(jnp.int32, (size, tile), 0) == wanted).astype(F32).astype(BF16)
        for part in range(2):
            chi[part, pl.ds(start, tile), :] = lax.dot_general(
                chosen, raw[part], (((0,), (0,)), ((), ())), preferred_element_type=F32
            ).astype(BF16)
        return carry

    lax.fori_loop(0, size // tile, reorder, 0)

    def forward(block, step):
        at_p = group * team + (t + step) % team
        ref = w_target(block, t)
        return remote(ref, ref, f_sent.at[block * team + step], f_got.at[block * team + step], at_p, r)

    def pass_on(k, carry):
        block = (r + k) % rows
        arrived(w_target(block, t), w_got.at[block])
        for step in range(1, team):
            forward(block, step).start()
        return carry

    def hand(block, step):
        at_p = group * team + (t + step) % team
        return remote(
            half_out.at[step - 1, block], half.at[t, block],
            h_sent.at[block * team + step], h_got.at[block * team + step], at_p, r,
        )

    width = min(tile, own_cols)

    def first(k, carry):
        block = (r + k) % rows
        pass_on(k, carry)
        for step in range(1, team):
            arrived(w_target(block, (t + team - step) % team), f_got.at[block * team + step])
        for step in range(team):
            part = (t + step) % team
            start = pl.multiple_of(block * w_rows + part * w_part, w_part)
            both = jnp.concatenate(
                (weight[0, pl.ds(start, w_part), :], weight[1, pl.ds(start, w_part), :]), axis=0
            )
            for c in range(own_cols // width):
                cols = slice(c * width, (c + 1) * width)
                by_real = jnp.dot(both, chi[0, :, cols], preferred_element_type=F32)
                by_imag = jnp.dot(both, chi[1, :, cols], preferred_element_type=F32)
                real = (by_real[:w_part] - by_imag[w_part:]).astype(BF16)
                imag = (by_imag[:w_part] + by_real[w_part:]).astype(BF16)
                value = jnp.concatenate((real, imag), axis=0)
                if step == 0:
                    half[t, block, :, cols] = value
                else:
                    half_out[step - 1, block, :, cols] = value
        for step in range(1, team):
            hand(block, step).start()
        return carry

    lax.fori_loop(0, rows, first, 0)

    def out_send(k, m):
        at_r = far_first(k)
        send(stage.at[at_r, m], out.at[slot], o_sent.at[at_r * dests + m], o_got.at[slot], t * dests + m, at_r)

    def second(k, carry):
        block = far_first(k)
        for step in range(1, team):
            arrived(half.at[(t + team - step) % team, block], h_got.at[block * team + step])

        def columns(c, inner):
            start = pl.multiple_of(c * tile, tile)
            by_real = jnp.zeros((2 * w_part, tile), F32)
            by_imag = jnp.zeros((2 * w_part, tile), F32)
            for source in range(team):
                left_side = half[source, block]
                deep = slice(source * own_cols, (source + 1) * own_cols)
                by_real += jnp.dot(left_side, weight[0, deep, pl.ds(start, tile)], preferred_element_type=F32)
                by_imag += jnp.dot(left_side, weight[1, deep, pl.ds(start, tile)], preferred_element_type=F32)
            real = (by_real[:w_part] - by_imag[w_part:]).astype(BF16)
            imag = (by_imag[:w_part] + by_real[w_part:]).astype(BF16)
            for m in range(dests):
                lines = slice(m * out_rows, (m + 1) * out_rows)
                stage[block, m, 0, :, pl.ds(start, tile)] = real[lines]
                stage[block, m, 1, :, pl.ds(start, tile)] = imag[lines]
            return inner

        lax.fori_loop(0, size // tile, columns, 0)

        @pl.when(k > 0)
        def _():
            for m in range(dests):
                out_send(k - 1, m)
        return carry

    lax.fori_loop(0, rows, second, 0)
    for m in range(dests):
        out_send(rows - 1, m)

    def out_wait(k, carry):
        arrived(out.at[k], o_got.at[k])
        return carry

    lax.fori_loop(0, slots, out_wait, 0)

    @pl.when(t == holder)
    def _():
        for step in range(1, team):
            pltpu.make_async_copy(mine, mine, g_sent.at[step - 1]).wait()

    def chi_left(k, carry):
        number, at_p, at_r = chi_place(k)
        left(response.at[number], chi_sent.at[k], at_p, at_r)
        return carry

    lax.fori_loop(0, slots, chi_left, 0)

    def w_left(k, carry):
        i, part, at_p, at_r = w_place(k)
        left(w_target(r, part), w_sent.at[k], at_p, at_r)
        return carry

    lax.fori_loop(0, per_pb * team, w_left, 0)

    def blocks_left(block, carry):
        for step in range(1, team):
            forward(block, step).wait_send()
            hand(block, step).wait_send()
        for m in range(dests):
            left(stage.at[block, m], o_sent.at[block * dests + m], t * dests + m, block)
        return carry

    lax.fori_loop(0, rows, blocks_left, 0)


def body(pb, rows, screened, response, q_owner, g_index):
    slots, _, block_rows, block_cols = response.shape
    per_pb, size = screened.shape[0], screened.shape[3]
    team = pb * rows // slots
    own_cols = size // team
    w_part = size // rows // team
    out_rows = size // (pb * rows)
    dests = pb // team
    spread = rows // team
    tile = min(256, size)

    def reordered(kernel, array, dtype, back):
        shape = (1,) + array.shape[1:]
        here = lambda q, order: (q, 0, 0, 0)
        there = lambda q, order: (order[q], 0, 0, 0)
        return pl.pallas_call(
            kernel,
            out_shape=jax.ShapeDtypeStruct(array.shape, dtype),
            grid_spec=pltpu.PrefetchScalarGridSpec(
                num_scalar_prefetch=1,
                grid=(slots,),
                in_specs=[pl.BlockSpec(shape, there if back else here)],
                out_specs=pl.BlockSpec(shape, here if back else there),
            ),
        )(q_owner, array)

    ordered = reordered(to_slots, response, response.dtype, False)
    dma = pltpu.SemaphoreType.DMA
    received = pl.pallas_call(
        functools.partial(team_kernel, pb, rows, team, tile),
        out_shape=jax.ShapeDtypeStruct((slots, 2, out_rows, size), BF16),
        in_specs=[pl.BlockSpec(memory_space=pl.ANY)] * 3,
        out_specs=pl.BlockSpec(memory_space=pl.ANY),
        scratch_shapes=[
            pltpu.VMEM((2, size, own_cols), BF16),
            pltpu.VMEM((2, size, size), BF16),
            pltpu.VMEM((2, size, own_cols), BF16),
            pltpu.VMEM((1, size), jnp.int32),
            pltpu.VMEM((team, rows, 2 * w_part, own_cols), BF16),
            pltpu.VMEM((max(team - 1, 1), rows, 2 * w_part, own_cols), BF16),
            pltpu.VMEM((rows, dests, 2, out_rows, size), BF16),
            dma((slots,)),
            dma((pb * spread,)),
            dma((per_pb * team,)),
            dma((rows,)),
            dma((rows * team,)),
            dma((rows * team,)),
            dma((team,)),
            dma(()),
            dma((rows * team,)),
            dma((rows * team,)),
            dma((rows * dests,)),
            dma((slots,)),
        ],
        compiler_params=pltpu.CompilerParams(
            collective_id=0, has_side_effects=True, vmem_limit_bytes=40 * 1024 * 1024
        ),
    )(ordered, screened, g_index.reshape(per_pb, 1, size))
    return reordered(from_slots, received, F32, True)


def solution(mesh):
    return jax.shard_map(
        functools.partial(body, mesh.shape["pb"], mesh.shape["row"]),
        mesh=mesh,
        in_specs=(P("pb", None, "row", None), P(None, None, "pb", "row"), P(), P("pb", None)),
        out_specs=P(None, None, ("row", "pb"), None),
        check_vma=False,
    )
```

```python
import functools

import jax
import jax.numpy as jnp
from jax import lax
from jax.experimental import pallas as pl
from jax.experimental.pallas import tpu as pltpu
from jax.sharding import PartitionSpec as P

F32 = jnp.float32
BF16 = jnp.bfloat16


def from_slots(count, order, source, target):
    for i in range(count):
        target[i] = source[order[pl.program_id(0) * count + i]].astype(target.dtype)


def team_kernel(
    pb, rows, team, tile,
    order, unordered, screened, table, out,
    loaded, response, own_table, raw, weight, chi, owner_table, half, half_out, stage,
    load_got, chi_sent, chi_got, w_sent, w_got, f_sent, f_got, g_sent, g_got, h_sent, h_got, o_sent, o_got,
):
    slots = response.shape[0]
    per_pb = screened.shape[0]
    size = screened.shape[3]
    groups = pb // team
    block_rows, block_cols = response.shape[2], response.shape[3]
    own_cols = size // team
    w_rows = size // rows
    w_part = w_rows // team
    spread = rows // team
    dests = pb // team
    out_rows = out.shape[2]
    near = rows // 2

    p, r = lax.axis_index("pb"), lax.axis_index("row")
    t, group = p % team, p // team
    slot = group * rows + r

    def same(a, b):
        return jnp.logical_and(a == p, b == r)

    load = pltpu.make_async_copy(unordered, loaded, load_got)
    load.start()
    barrier = pltpu.get_barrier_semaphore()

    def greet(k, carry):
        @pl.when(k != p * rows + r)
        def _():
            pl.semaphore_signal(barrier, inc=1, device_id=(k // rows, k % rows), device_id_type=pl.DeviceIdType.MESH)
        return carry

    lax.fori_loop(0, pb * rows, greet, 0)

    for i in range(per_pb):
        @pl.when(r % per_pb == i)
        def _():
            own_table[...] = table[i : i + 1, :]

    load.wait()

    def arrange(number, carry):
        q = 0
        for i in range(1, slots):
            q = jnp.where(order[i] == number, i, q)
        response[number] = loaded[q]
        return carry

    lax.fori_loop(0, slots, arrange, 0)
    pl.semaphore_wait(barrier, pb * rows - 1)

    def send(src, dst, sent, got, at_p, at_r):
        @pl.when(same(at_p, at_r))
        def _():
            pltpu.make_async_copy(src, dst, got).start()

        @pl.when(jnp.logical_not(same(at_p, at_r)))
        def _():
            remote(src, dst, sent, got, at_p, at_r).start()

    def remote(src, dst, sent, got, at_p, at_r):
        return pltpu.make_async_remote_copy(
            src_ref=src, dst_ref=dst, send_sem=sent, recv_sem=got,
            device_id=(at_p, at_r), device_id_type=pl.DeviceIdType.MESH,
        )

    def arrived(ref, sem):
        pltpu.make_async_copy(ref, ref, sem).wait()

    def left(ref, sem, at_p, at_r):
        @pl.when(jnp.logical_not(same(at_p, at_r)))
        def _():
            pltpu.make_async_copy(ref, ref, sem).wait()

    def far_first(k):
        side = r // near
        across = (1 - side) * near + (r + k) % near
        beside = side * near + (r + 1 + k) % near
        return jnp.where(k < near, across, beside)

    holder = r // per_pb
    @pl.when(t == holder)
    def _():
        pltpu.make_async_copy(own_table, owner_table, g_got).start()
        for step in range(1, team):
            remote(own_table, owner_table, g_sent.at[step - 1], g_got, group * team + (t + step) % team, r).start()

    member = r // spread

    def chi_place(k):
        at_r = far_first(k // groups)
        at_group = (group + k) % groups
        return at_group * rows + at_r, at_group * team + member, at_r

    def chi_target(from_p, from_r):
        return raw.at[
            :,
            pl.ds(pl.multiple_of(from_p * block_rows, block_rows), block_rows),
            pl.ds(pl.multiple_of((from_r % spread) * block_cols, block_cols), block_cols),
        ]

    def chi_send(k, carry):
        number, at_p, at_r = chi_place(k)
        send(response.at[number], chi_target(p, r), chi_sent.at[k], chi_got.at[p * spread + r % spread], at_p, at_r)
        return carry

    lax.fori_loop(0, slots, chi_send, 0)

    def w_target(block, part):
        start = pl.multiple_of(block * w_rows + part * w_part, w_part)
        return weight.at[:, pl.ds(start, w_part), :]

    def w_place(k):
        i, part = k // team, k % team
        return i, part, group * team + part, t * per_pb + i

    def w_send(k, carry):
        i, part, at_p, at_r = w_place(k)
        src = screened.at[i, :, pl.ds(pl.multiple_of(part * w_part, w_part), w_part), :]
        send(src, w_target(r, part), w_sent.at[k], w_got.at[r], at_p, at_r)
        return carry

    lax.fori_loop(0, per_pb * team, w_send, 0)

    arrived(owner_table, g_got)

    def chi_wait(k, carry):
        arrived(chi_target(k // spread, k % spread), chi_got.at[k])
        return carry

    lax.fori_loop(0, pb * spread, chi_wait, 0)

    def reorder(k, carry):
        start = pl.multiple_of(k * tile, tile)
        wanted = owner_table[:, pl.ds(start, tile)]
        chosen = (lax.broadcasted_iota(jnp.int32, (size, tile), 0) == wanted).astype(F32).astype(BF16)
        for part in range(2):
            chi[part, pl.ds(start, tile), :] = lax.dot_general(
                chosen, raw[part], (((0,), (0,)), ((), ())), preferred_element_type=F32
            ).astype(BF16)
        return carry

    lax.fori_loop(0, size // tile, reorder, 0)

    def forward(block, step):
        at_p = group * team + (t + step) % team
        ref = w_target(block, t)
        return remote(ref, ref, f_sent.at[block * team + step], f_got.at[block * team + step], at_p, r)

    def take(block):
        arrived(w_target(block, t), w_got.at[block])
        for step in range(1, team):
            forward(block, step).start()
        for step in range(1, team):
            arrived(w_target(block, (t + team - step) % team), f_got.at[block * team + step])

    def hand(block, step):
        at_p = group * team + (t + step) % team
        return remote(
            half_out.at[step - 1, block], half.at[t, block],
            h_sent.at[block * team + step], h_got.at[block * team + step], at_p, r,
        )

    width = min(tile, own_cols)

    def first(block):
        for step in range(1, team + 1):
            part = (t + step) % team
            start = pl.multiple_of(block * w_rows + part * w_part, w_part)
            both = jnp.concatenate(
                (weight[0, pl.ds(start, w_part), :], weight[1, pl.ds(start, w_part), :]), axis=0
            )
            for c in range(own_cols // width):
                cols = slice(c * width, (c + 1) * width)
                by_real = jnp.dot(both, chi[0, :, cols], preferred_element_type=F32)
                by_imag = jnp.dot(both, chi[1, :, cols], preferred_element_type=F32)
                real = (by_real[:w_part] - by_imag[w_part:]).astype(BF16)
                imag = (by_imag[:w_part] + by_real[w_part:]).astype(BF16)
                value = jnp.concatenate((real, imag), axis=0)
                if step == team:
                    half[t, block, :, cols] = value
                else:
                    half_out[step - 1, block, :, cols] = value
            if step < team:
                hand(block, step).start()

    def out_send(k, m):
        at_r = far_first(k)
        send(stage.at[at_r, m], out.at[slot], o_sent.at[at_r * dests + m], o_got.at[slot], t * dests + m, at_r)

    def second(k):
        block = far_first(k)
        for step in range(1, team):
            arrived(half.at[(t + team - step) % team, block], h_got.at[block * team + step])

        def columns(c, inner):
            start = pl.multiple_of(c * tile, tile)
            by_real = jnp.zeros((2 * w_part, tile), F32)
            by_imag = jnp.zeros((2 * w_part, tile), F32)
            for source in range(team):
                left_side = half[source, block]
                deep = slice(source * own_cols, (source + 1) * own_cols)
                by_real += jnp.dot(left_side, weight[0, deep, pl.ds(start, tile)], preferred_element_type=F32)
                by_imag += jnp.dot(left_side, weight[1, deep, pl.ds(start, tile)], preferred_element_type=F32)
            real = (by_real[:w_part] - by_imag[w_part:]).astype(BF16)
            imag = (by_imag[:w_part] + by_real[w_part:]).astype(BF16)
            for m in range(dests):
                lines = slice(m * out_rows, (m + 1) * out_rows)
                stage[block, m, 0, :, pl.ds(start, tile)] = real[lines]
                stage[block, m, 1, :, pl.ds(start, tile)] = imag[lines]
            return inner

        lax.fori_loop(0, size // tile, columns, 0)

        for m in range(dests):
            out_send(k, m)

    def near_first(k, carry):
        block = far_first(rows - 1 - k)
        take(block)
        first(block)
        return carry

    lax.fori_loop(0, rows - 1, near_first, 0)
    take(far_first(0))

    def finish(k, carry):
        @pl.when(k == 1)
        def _():
            first(far_first(0))

        second(jnp.where(k < 2, 1 - k, k))
        return carry

    lax.fori_loop(0, rows, finish, 0)

    def out_wait(k, carry):
        arrived(out.at[k], o_got.at[k])
        return carry

    lax.fori_loop(0, slots, out_wait, 0)

    @pl.when(t == holder)
    def _():
        for step in range(1, team):
            pltpu.make_async_copy(own_table, own_table, g_sent.at[step - 1]).wait()

    def chi_left(k, carry):
        number, at_p, at_r = chi_place(k)
        left(response.at[number], chi_sent.at[k], at_p, at_r)
        return carry

    lax.fori_loop(0, slots, chi_left, 0)

    def w_left(k, carry):
        i, part, at_p, at_r = w_place(k)
        left(w_target(r, part), w_sent.at[k], at_p, at_r)
        return carry

    lax.fori_loop(0, per_pb * team, w_left, 0)

    def blocks_left(block, carry):
        for step in range(1, team):
            forward(block, step).wait_send()
            hand(block, step).wait_send()
        for m in range(dests):
            left(stage.at[block, m], o_sent.at[block * dests + m], t * dests + m, block)
        return carry

    lax.fori_loop(0, rows, blocks_left, 0)


def body(pb, rows, screened, response, q_owner, g_index):
    slots, _, block_rows, block_cols = response.shape
    per_pb, size = screened.shape[0], screened.shape[3]
    team = pb * rows // slots
    own_cols = size // team
    w_part = size // rows // team
    out_rows = size // (pb * rows)
    dests = pb // team
    spread = rows // team
    tile = min(256, size)

    dma = pltpu.SemaphoreType.DMA
    received = pl.pallas_call(
        functools.partial(team_kernel, pb, rows, team, tile),
        out_shape=jax.ShapeDtypeStruct((slots, 2, out_rows, size), BF16),
        in_specs=[
            pl.BlockSpec(memory_space=pltpu.SMEM),
            pl.BlockSpec(memory_space=pl.ANY),
            pl.BlockSpec(memory_space=pl.ANY),
            pl.BlockSpec(memory_space=pltpu.VMEM),
        ],
        out_specs=pl.BlockSpec(memory_space=pl.ANY),
        scratch_shapes=[
            pltpu.VMEM(response.shape, BF16),
            pltpu.VMEM(response.shape, BF16),
            pltpu.VMEM((1, size), jnp.int32),
            pltpu.VMEM((2, size, own_cols), BF16),
            pltpu.VMEM((2, size, size), BF16),
            pltpu.VMEM((2, size, own_cols), BF16),
            pltpu.VMEM((1, size), jnp.int32),
            pltpu.VMEM((team, rows, 2 * w_part, own_cols), BF16),
            pltpu.VMEM((max(team - 1, 1), rows, 2 * w_part, own_cols), BF16),
            pltpu.VMEM((rows, dests, 2, out_rows, size), BF16),
            dma(()),
            dma((slots,)),
            dma((pb * spread,)),
            dma((per_pb * team,)),
            dma((rows,)),
            dma((rows * team,)),
            dma((rows * team,)),
            dma((team,)),
            dma(()),
            dma((rows * team,)),
            dma((rows * team,)),
            dma((rows * dests,)),
            dma((slots,)),
        ],
        compiler_params=pltpu.CompilerParams(
            collective_id=0, has_side_effects=True, vmem_limit_bytes=60 * 1024 * 1024
        ),
    )(q_owner, response, screened, g_index)
    count = slots // 4
    return pl.pallas_call(
        functools.partial(from_slots, count),
        out_shape=jax.ShapeDtypeStruct(received.shape, F32),
        grid_spec=pltpu.PrefetchScalarGridSpec(
            num_scalar_prefetch=1,
            grid=(slots // count,),
            in_specs=[pl.BlockSpec(received.shape, lambda q, order: (0, 0, 0, 0), pipeline_mode=pl.Buffered(1))],
            out_specs=pl.BlockSpec((count,) + received.shape[1:], lambda q, order: (q, 0, 0, 0)),
        ),
    )(q_owner, received)


def solution(mesh):
    return jax.shard_map(
        functools.partial(body, mesh.shape["pb"], mesh.shape["row"]),
        mesh=mesh,
        in_specs=(P("pb", None, "row", None), P(None, None, "pb", "row"), P(), P("pb", None)),
        out_specs=P(None, None, ("row", "pb"), None),
        check_vma=False,
    )
```

```python
import functools

import jax
import jax.numpy as jnp
from jax import lax
from jax.experimental import pallas as pl
from jax.experimental.pallas import tpu as pltpu
from jax.sharding import PartitionSpec as P

F32 = jnp.float32
BF16 = jnp.bfloat16


def from_slots(count, order, source, target):
    for i in range(count):
        target[i] = source[order[pl.program_id(0) * count + i]].astype(target.dtype)


def team_kernel(
    pb, rows, team, tile,
    order, unordered, screened, table, out,
    loaded, response, own_table, raw, weight, chi, owner_table, half, half_out, stage,
    load_got, chi_sent, chi_got, w_sent, w_got, f_sent, f_got, g_sent, g_got, h_sent, h_got, o_sent, o_got,
):
    slots = response.shape[0]
    per_pb = screened.shape[0]
    size = screened.shape[3]
    groups = pb // team
    block_rows, block_cols = response.shape[2], response.shape[3]
    own_cols = size // team
    w_rows = size // rows
    w_part = w_rows // team
    spread = rows // team
    dests = pb // team
    out_rows = out.shape[2]
    near = rows // 2

    p, r = lax.axis_index("pb"), lax.axis_index("row")
    t, group = p % team, p // team
    slot = group * rows + r

    def same(a, b):
        return jnp.logical_and(a == p, b == r)

    load = pltpu.make_async_copy(unordered, loaded, load_got)
    load.start()
    barrier = pltpu.get_barrier_semaphore()

    def greet(k, carry):
        @pl.when(k != p * rows + r)
        def _():
            pl.semaphore_signal(barrier, inc=1, device_id=(k // rows, k % rows), device_id_type=pl.DeviceIdType.MESH)
        return carry

    lax.fori_loop(0, pb * rows, greet, 0)

    for i in range(per_pb):
        @pl.when(r % per_pb == i)
        def _():
            own_table[...] = table[i : i + 1, :]

    load.wait()

    def arrange(number, carry):
        q = 0
        for i in range(1, slots):
            q = jnp.where(order[i] == number, i, q)
        response[number] = loaded[q]
        return carry

    lax.fori_loop(0, slots, arrange, 0)
    pl.semaphore_wait(barrier, pb * rows - 1)

    def send(src, dst, sent, got, at_p, at_r):
        @pl.when(same(at_p, at_r))
        def _():
            pltpu.make_async_copy(src, dst, got).start()

        @pl.when(jnp.logical_not(same(at_p, at_r)))
        def _():
            remote(src, dst, sent, got, at_p, at_r).start()

    def remote(src, dst, sent, got, at_p, at_r):
        return pltpu.make_async_remote_copy(
            src_ref=src, dst_ref=dst, send_sem=sent, recv_sem=got,
            device_id=(at_p, at_r), device_id_type=pl.DeviceIdType.MESH,
        )

    def arrived(ref, sem):
        pltpu.make_async_copy(ref, ref, sem).wait()

    def left(ref, sem, at_p, at_r):
        @pl.when(jnp.logical_not(same(at_p, at_r)))
        def _():
            pltpu.make_async_copy(ref, ref, sem).wait()

    def far_first(k):
        side = r // near
        across = (1 - side) * near + (r + k) % near
        beside = side * near + (r + 1 + k) % near
        return jnp.where(k < near, across, beside)

    holder = r // per_pb
    @pl.when(t == holder)
    def _():
        pltpu.make_async_copy(own_table, owner_table, g_got).start()
        for step in range(1, team):
            remote(own_table, owner_table, g_sent.at[step - 1], g_got, group * team + (t + step) % team, r).start()

    def w_target(block, part):
        start = pl.multiple_of(block * w_rows + part * w_part, w_part)
        return weight.at[:, pl.ds(start, w_part), :]

    def w_place(k):
        i, part = k // team, k % team
        return i, part, group * team + part, t * per_pb + i

    def w_send(k, carry):
        i, part, at_p, at_r = w_place(k)
        src = screened.at[i, :, pl.ds(pl.multiple_of(part * w_part, w_part), w_part), :]
        send(src, w_target(r, part), w_sent.at[k], w_got.at[r], at_p, at_r)
        return carry


    lax.fori_loop(0, per_pb * team, w_send, 0)

    member = r // spread

    def chi_place(k):
        at_r = far_first(k // groups)
        at_group = (group + k) % groups
        return at_group * rows + at_r, at_group * team + member, at_r

    def chi_target(from_p, from_r):
        return raw.at[
            :,
            pl.ds(pl.multiple_of(from_p * block_rows, block_rows), block_rows),
            pl.ds(pl.multiple_of((from_r % spread) * block_cols, block_cols), block_cols),
        ]

    def chi_send(k, carry):
        number, at_p, at_r = chi_place(k)
        send(response.at[number], chi_target(p, r), chi_sent.at[k], chi_got.at[p * spread + r % spread], at_p, at_r)
        return carry

    lax.fori_loop(0, slots, chi_send, 0)

    arrived(owner_table, g_got)

    def chi_wait(k, carry):
        arrived(chi_target(k // spread, k % spread), chi_got.at[k])
        return carry

    lax.fori_loop(0, pb * spread, chi_wait, 0)

    def reorder(k, carry):
        start = pl.multiple_of(k * tile, tile)
        wanted = owner_table[:, pl.ds(start, tile)]
        chosen = (lax.broadcasted_iota(jnp.int32, (size, tile), 0) == wanted).astype(F32).astype(BF16)
        for part in range(2):
            chi[part, pl.ds(start, tile), :] = lax.dot_general(
                chosen, raw[part], (((0,), (0,)), ((), ())), preferred_element_type=F32
            ).astype(BF16)
        return carry

    lax.fori_loop(0, size // tile, reorder, 0)

    def forward(block, step):
        at_p = group * team + (t + step) % team
        ref = w_target(block, t)
        return remote(ref, ref, f_sent.at[block * team + step], f_got.at[block * team + step], at_p, r)

    def take(block):
        arrived(w_target(block, t), w_got.at[block])
        for step in range(1, team):
            forward(block, step).start()
        for step in range(1, team):
            arrived(w_target(block, (t + team - step) % team), f_got.at[block * team + step])

    def hand(block, step):
        at_p = group * team + (t + step) % team
        return remote(
            half_out.at[step - 1, block], half.at[t, block],
            h_sent.at[block * team + step], h_got.at[block * team + step], at_p, r,
        )

    width = min(tile, own_cols)

    def first(block):
        for step in range(1, team + 1):
            part = (t + step) % team
            start = pl.multiple_of(block * w_rows + part * w_part, w_part)
            both = jnp.concatenate(
                (weight[0, pl.ds(start, w_part), :], weight[1, pl.ds(start, w_part), :]), axis=0
            )
            for c in range(own_cols // width):
                cols = slice(c * width, (c + 1) * width)
                by_real = jnp.dot(both, chi[0, :, cols], preferred_element_type=F32)
                by_imag = jnp.dot(both, chi[1, :, cols], preferred_element_type=F32)
                real = (by_real[:w_part] - by_imag[w_part:]).astype(BF16)
                imag = (by_imag[:w_part] + by_real[w_part:]).astype(BF16)
                value = jnp.concatenate((real, imag), axis=0)
                if step == team:
                    half[t, block, :, cols] = value
                else:
                    half_out[step - 1, block, :, cols] = value
            if step < team:
                hand(block, step).start()

    def in_turn(k, carry):
        block = (r + k) % rows
        take(block)
        first(block)
        return carry

    lax.fori_loop(0, rows, in_turn, 0)

    def out_send(k, m):
        at_r = far_first(k)
        send(stage.at[at_r, m], out.at[slot], o_sent.at[at_r * dests + m], o_got.at[slot], t * dests + m, at_r)

    def second(k, carry):
        block = far_first(k)
        for step in range(1, team):
            arrived(half.at[(t + team - step) % team, block], h_got.at[block * team + step])

        def columns(c, inner):
            start = pl.multiple_of(c * tile, tile)
            by_real = jnp.zeros((2 * w_part, tile), F32)
            by_imag = jnp.zeros((2 * w_part, tile), F32)
            for source in range(team):
                left_side = half[source, block]
                deep = slice(source * own_cols, (source + 1) * own_cols)
                by_real += jnp.dot(left_side, weight[0, deep, pl.ds(start, tile)], preferred_element_type=F32)
                by_imag += jnp.dot(left_side, weight[1, deep, pl.ds(start, tile)], preferred_element_type=F32)
            real = (by_real[:w_part] - by_imag[w_part:]).astype(BF16)
            imag = (by_imag[:w_part] + by_real[w_part:]).astype(BF16)
            for m in range(dests):
                lines = slice(m * out_rows, (m + 1) * out_rows)
                stage[block, m, 0, :, pl.ds(start, tile)] = real[lines]
                stage[block, m, 1, :, pl.ds(start, tile)] = imag[lines]
            return inner

        lax.fori_loop(0, size // tile, columns, 0)

        @pl.when(k > 0)
        def _():
            for m in range(dests):
                out_send(k - 1, m)
        return carry

    lax.fori_loop(0, rows, second, 0)
    for m in range(dests):
        out_send(rows - 1, m)

    def out_wait(k, carry):
        arrived(out.at[k], o_got.at[k])
        return carry

    lax.fori_loop(0, slots, out_wait, 0)

    @pl.when(t == holder)
    def _():
        for step in range(1, team):
            pltpu.make_async_copy(own_table, own_table, g_sent.at[step - 1]).wait()

    def chi_left(k, carry):
        number, at_p, at_r = chi_place(k)
        left(response.at[number], chi_sent.at[k], at_p, at_r)
        return carry

    lax.fori_loop(0, slots, chi_left, 0)

    def w_left(k, carry):
        i, part, at_p, at_r = w_place(k)
        left(w_target(r, part), w_sent.at[k], at_p, at_r)
        return carry

    lax.fori_loop(0, per_pb * team, w_left, 0)

    def blocks_left(block, carry):
        for step in range(1, team):
            forward(block, step).wait_send()
            hand(block, step).wait_send()
        for m in range(dests):
            left(stage.at[block, m], o_sent.at[block * dests + m], t * dests + m, block)
        return carry

    lax.fori_loop(0, rows, blocks_left, 0)


def body(pb, rows, screened, response, q_owner, g_index):
    slots, _, block_rows, block_cols = response.shape
    per_pb, size = screened.shape[0], screened.shape[3]
    team = pb * rows // slots
    own_cols = size // team
    w_part = size // rows // team
    out_rows = size // (pb * rows)
    dests = pb // team
    spread = rows // team
    tile = min(256, size)

    dma = pltpu.SemaphoreType.DMA
    received = pl.pallas_call(
        functools.partial(team_kernel, pb, rows, team, tile),
        out_shape=jax.ShapeDtypeStruct((slots, 2, out_rows, size), BF16),
        in_specs=[
            pl.BlockSpec(memory_space=pltpu.SMEM),
            pl.BlockSpec(memory_space=pl.ANY),
            pl.BlockSpec(memory_space=pl.ANY),
            pl.BlockSpec(memory_space=pltpu.VMEM),
        ],
        out_specs=pl.BlockSpec(memory_space=pl.ANY),
        scratch_shapes=[
            pltpu.VMEM(response.shape, BF16),
            pltpu.VMEM(response.shape, BF16),
            pltpu.VMEM((1, size), jnp.int32),
            pltpu.VMEM((2, size, own_cols), BF16),
            pltpu.VMEM((2, size, size), BF16),
            pltpu.VMEM((2, size, own_cols), BF16),
            pltpu.VMEM((1, size), jnp.int32),
            pltpu.VMEM((team, rows, 2 * w_part, own_cols), BF16),
            pltpu.VMEM((max(team - 1, 1), rows, 2 * w_part, own_cols), BF16),
            pltpu.VMEM((rows, dests, 2, out_rows, size), BF16),
            dma(()),
            dma((slots,)),
            dma((pb * spread,)),
            dma((per_pb * team,)),
            dma((rows,)),
            dma((rows * team,)),
            dma((rows * team,)),
            dma((team,)),
            dma(()),
            dma((rows * team,)),
            dma((rows * team,)),
            dma((rows * dests,)),
            dma((slots,)),
        ],
        compiler_params=pltpu.CompilerParams(
            collective_id=0, has_side_effects=True, vmem_limit_bytes=60 * 1024 * 1024
        ),
    )(q_owner, response, screened, g_index)
    count = slots // 4
    return pl.pallas_call(
        functools.partial(from_slots, count),
        out_shape=jax.ShapeDtypeStruct(received.shape, F32),
        grid_spec=pltpu.PrefetchScalarGridSpec(
            num_scalar_prefetch=1,
            grid=(slots // count,),
            in_specs=[pl.BlockSpec(received.shape, lambda q, order: (0, 0, 0, 0), pipeline_mode=pl.Buffered(1))],
            out_specs=pl.BlockSpec((count,) + received.shape[1:], lambda q, order: (q, 0, 0, 0)),
        ),
    )(q_owner, received)


def solution(mesh):
    return jax.shard_map(
        functools.partial(body, mesh.shape["pb"], mesh.shape["row"]),
        mesh=mesh,
        in_specs=(P("pb", None, "row", None), P(None, None, "pb", "row"), P(), P("pb", None)),
        out_specs=P(None, None, ("row", "pb"), None),
        check_vma=False,
    )
```

```python
import functools

import jax
import jax.numpy as jnp
from jax import lax
from jax.experimental import pallas as pl
from jax.experimental.pallas import tpu as pltpu
from jax.sharding import PartitionSpec as P

F32 = jnp.float32
BF16 = jnp.bfloat16


def from_slots(count, order, source, target):
    for i in range(count):
        target[i] = source[order[pl.program_id(0) * count + i]].astype(target.dtype)


def team_kernel(
    pb, rows, team, tile,
    order, unordered, screened, table, out,
    loaded, response, own_table, raw, weight, turned, owner_table, half, half_out, stage,
    load_got, chi_sent, chi_got, w_sent, w_got, f_sent, f_got, g_sent, g_got, h_sent, h_got, o_sent, o_got,
):
    slots = response.shape[0]
    per_pb = screened.shape[0]
    size = screened.shape[3]
    groups = pb // team
    block_rows, block_cols = response.shape[2], response.shape[3]
    own_cols = size // team
    w_rows = size // rows
    w_part = w_rows // team
    spread = rows // team
    dests = pb // team
    out_rows = out.shape[2]
    near = rows // 2

    p, r = lax.axis_index("pb"), lax.axis_index("row")
    t, group = p % team, p // team
    slot = group * rows + r

    def same(a, b):
        return jnp.logical_and(a == p, b == r)

    load = pltpu.make_async_copy(unordered, loaded, load_got)
    load.start()
    barrier = pltpu.get_barrier_semaphore()

    def greet(k, carry):
        @pl.when(k != p * rows + r)
        def _():
            pl.semaphore_signal(barrier, inc=1, device_id=(k // rows, k % rows), device_id_type=pl.DeviceIdType.MESH)
        return carry

    lax.fori_loop(0, pb * rows, greet, 0)

    for i in range(per_pb):
        @pl.when(r % per_pb == i)
        def _():
            own_table[...] = table[i : i + 1, :]

    load.wait()

    def arrange(number, carry):
        q = 0
        for i in range(1, slots):
            q = jnp.where(order[i] == number, i, q)
        response[number] = loaded[q]
        return carry

    lax.fori_loop(0, slots, arrange, 0)
    pl.semaphore_wait(barrier, pb * rows - 1)

    def send(src, dst, sent, got, at_p, at_r):
        @pl.when(same(at_p, at_r))
        def _():
            pltpu.make_async_copy(src, dst, got).start()

        @pl.when(jnp.logical_not(same(at_p, at_r)))
        def _():
            remote(src, dst, sent, got, at_p, at_r).start()

    def remote(src, dst, sent, got, at_p, at_r):
        return pltpu.make_async_remote_copy(
            src_ref=src, dst_ref=dst, send_sem=sent, recv_sem=got,
            device_id=(at_p, at_r), device_id_type=pl.DeviceIdType.MESH,
        )

    def arrived(ref, sem):
        pltpu.make_async_copy(ref, ref, sem).wait()

    def left(ref, sem, at_p, at_r):
        @pl.when(jnp.logical_not(same(at_p, at_r)))
        def _():
            pltpu.make_async_copy(ref, ref, sem).wait()

    def far_first(k):
        side = r // near
        across = (1 - side) * near + (r + k) % near
        beside = side * near + (r + 1 + k) % near
        return jnp.where(k < near, across, beside)

    holder = r // per_pb
    @pl.when(t == holder)
    def _():
        pltpu.make_async_copy(own_table, owner_table, g_got).start()
        for step in range(1, team):
            remote(own_table, owner_table, g_sent.at[step - 1], g_got, group * team + (t + step) % team, r).start()

    def w_target(block, part):
        start = pl.multiple_of(block * w_rows + part * w_part, w_part)
        return weight.at[:, pl.ds(start, w_part), :]

    def w_place(k):
        i, part = k // team, k % team
        return i, part, group * team + part, t * per_pb + i

    def w_send(k, carry):
        i, part, at_p, at_r = w_place(k)
        src = screened.at[i, :, pl.ds(pl.multiple_of(part * w_part, w_part), w_part), :]
        send(src, w_target(r, part), w_sent.at[k], w_got.at[r], at_p, at_r)
        return carry


    lax.fori_loop(0, per_pb * team, w_send, 0)

    member = r // spread

    def chi_place(k):
        at_r = far_first(k // groups)
        at_group = (group + k) % groups
        return at_group * rows + at_r, at_group * team + member, at_r

    def chi_target(from_p, from_r):
        return raw.at[
            :,
            pl.ds(pl.multiple_of(from_p * block_rows, block_rows), block_rows),
            pl.ds(pl.multiple_of((from_r % spread) * block_cols, block_cols), block_cols),
        ]

    def chi_send(k, carry):
        number, at_p, at_r = chi_place(k)
        send(response.at[number], chi_target(p, r), chi_sent.at[k], chi_got.at[p * spread + r % spread], at_p, at_r)
        return carry

    lax.fori_loop(0, slots, chi_send, 0)

    def forward(block, step):
        at_p = group * team + (t + step) % team
        ref = w_target(block, t)
        return remote(ref, ref, f_sent.at[block * team + step], f_got.at[block * team + step], at_p, r)

    def take(block):
        arrived(w_target(block, t), w_got.at[block])
        for step in range(1, team):
            forward(block, step).start()
        for step in range(1, team):
            arrived(w_target(block, (t + team - step) % team), f_got.at[block * team + step])

    def hand(block, step):
        at_p = group * team + (t + step) % team
        return remote(
            half_out.at[step - 1, block], half.at[t, block],
            h_sent.at[block * team + step], h_got.at[block * team + step], at_p, r,
        )

    width = min(tile, own_cols)

    def take_turn(k, carry):
        take((r + k) % rows)
        return carry

    lax.fori_loop(0, rows, take_turn, 0)
    arrived(owner_table, g_got)

    def reorder(k, carry):
        start = pl.multiple_of((k // 2) * tile, tile)
        wanted = lax.broadcasted_iota(jnp.int32, (tile, size), 0) + start
        chosen = (wanted == owner_table[...]).astype(F32).astype(BF16)
        turned[k % 2, :, pl.ds(start, tile)] = lax.dot_general(
            weight[k % 2], chosen, (((1,), (1,)), ((), ())), preferred_element_type=F32
        ).astype(BF16)
        return carry

    lax.fori_loop(0, 2 * (size // tile), reorder, 0)

    def chi_wait(k, carry):
        arrived(chi_target(k // spread, k % spread), chi_got.at[k])
        return carry

    lax.fori_loop(0, pb * spread, chi_wait, 0)

    def first(block):
        for step in range(1, team + 1):
            part = (t + step) % team
            start = pl.multiple_of(block * w_rows + part * w_part, w_part)
            both = jnp.concatenate(
                (turned[0, pl.ds(start, w_part), :], turned[1, pl.ds(start, w_part), :]), axis=0
            )
            for c in range(own_cols // width):
                cols = slice(c * width, (c + 1) * width)
                by_real = jnp.dot(both, raw[0, :, cols], preferred_element_type=F32)
                by_imag = jnp.dot(both, raw[1, :, cols], preferred_element_type=F32)
                real = (by_real[:w_part] - by_imag[w_part:]).astype(BF16)
                imag = (by_imag[:w_part] + by_real[w_part:]).astype(BF16)
                value = jnp.concatenate((real, imag), axis=0)
                if step == team:
                    half[t, block, :, cols] = value
                else:
                    half_out[step - 1, block, :, cols] = value
            if step < team:
                hand(block, step).start()

    def in_turn(k, carry):
        block = (r + k) % rows
        first(block)
        return carry

    lax.fori_loop(0, rows, in_turn, 0)

    def out_send(k, m):
        at_r = far_first(k)
        send(stage.at[at_r, m], out.at[slot], o_sent.at[at_r * dests + m], o_got.at[slot], t * dests + m, at_r)

    def second(k, carry):
        block = far_first(k)
        for step in range(1, team):
            arrived(half.at[(t + team - step) % team, block], h_got.at[block * team + step])

        def columns(c, inner):
            start = pl.multiple_of(c * tile, tile)
            by_real = jnp.zeros((2 * w_part, tile), F32)
            by_imag = jnp.zeros((2 * w_part, tile), F32)
            for source in range(team):
                left_side = half[source, block]
                deep = slice(source * own_cols, (source + 1) * own_cols)
                by_real += jnp.dot(left_side, weight[0, deep, pl.ds(start, tile)], preferred_element_type=F32)
                by_imag += jnp.dot(left_side, weight[1, deep, pl.ds(start, tile)], preferred_element_type=F32)
            real = (by_real[:w_part] - by_imag[w_part:]).astype(BF16)
            imag = (by_imag[:w_part] + by_real[w_part:]).astype(BF16)
            for m in range(dests):
                lines = slice(m * out_rows, (m + 1) * out_rows)
                stage[block, m, 0, :, pl.ds(start, tile)] = real[lines]
                stage[block, m, 1, :, pl.ds(start, tile)] = imag[lines]
            return inner

        lax.fori_loop(0, size // tile, columns, 0)

        @pl.when(k > 0)
        def _():
            for m in range(dests):
                out_send(k - 1, m)
        return carry

    lax.fori_loop(0, rows, second, 0)
    for m in range(dests):
        out_send(rows - 1, m)

    def out_wait(k, carry):
        arrived(out.at[k], o_got.at[k])
        return carry

    lax.fori_loop(0, slots, out_wait, 0)

    @pl.when(t == holder)
    def _():
        for step in range(1, team):
            pltpu.make_async_copy(own_table, own_table, g_sent.at[step - 1]).wait()

    def chi_left(k, carry):
        number, at_p, at_r = chi_place(k)
        left(response.at[number], chi_sent.at[k], at_p, at_r)
        return carry

    lax.fori_loop(0, slots, chi_left, 0)

    def w_left(k, carry):
        i, part, at_p, at_r = w_place(k)
        left(w_target(r, part), w_sent.at[k], at_p, at_r)
        return carry

    lax.fori_loop(0, per_pb * team, w_left, 0)

    def blocks_left(block, carry):
        for step in range(1, team):
            forward(block, step).wait_send()
            hand(block, step).wait_send()
        for m in range(dests):
            left(stage.at[block, m], o_sent.at[block * dests + m], t * dests + m, block)
        return carry

    lax.fori_loop(0, rows, blocks_left, 0)


def body(pb, rows, screened, response, q_owner, g_index):
    slots, _, block_rows, block_cols = response.shape
    per_pb, size = screened.shape[0], screened.shape[3]
    team = pb * rows // slots
    own_cols = size // team
    w_part = size // rows // team
    out_rows = size // (pb * rows)
    dests = pb // team
    spread = rows // team
    tile = min(256, size)

    dma = pltpu.SemaphoreType.DMA
    received = pl.pallas_call(
        functools.partial(team_kernel, pb, rows, team, tile),
        out_shape=jax.ShapeDtypeStruct((slots, 2, out_rows, size), BF16),
        in_specs=[
            pl.BlockSpec(memory_space=pltpu.SMEM),
            pl.BlockSpec(memory_space=pl.ANY),
            pl.BlockSpec(memory_space=pl.ANY),
            pl.BlockSpec(memory_space=pltpu.VMEM),
        ],
        out_specs=pl.BlockSpec(memory_space=pl.ANY),
        scratch_shapes=[
            pltpu.VMEM(response.shape, BF16),
            pltpu.VMEM(response.shape, BF16),
            pltpu.VMEM((1, size), jnp.int32),
            pltpu.VMEM((2, size, own_cols), BF16),
            pltpu.VMEM((2, size, size), BF16),
            pltpu.VMEM((2, size, size), BF16),
            pltpu.VMEM((1, size), jnp.int32),
            pltpu.VMEM((team, rows, 2 * w_part, own_cols), BF16),
            pltpu.VMEM((max(team - 1, 1), rows, 2 * w_part, own_cols), BF16),
            pltpu.VMEM((rows, dests, 2, out_rows, size), BF16),
            dma(()),
            dma((slots,)),
            dma((pb * spread,)),
            dma((per_pb * team,)),
            dma((rows,)),
            dma((rows * team,)),
            dma((rows * team,)),
            dma((team,)),
            dma(()),
            dma((rows * team,)),
            dma((rows * team,)),
            dma((rows * dests,)),
            dma((slots,)),
        ],
        compiler_params=pltpu.CompilerParams(
            collective_id=0, has_side_effects=True, vmem_limit_bytes=60 * 1024 * 1024
        ),
    )(q_owner, response, screened, g_index)
    count = slots // 4
    return pl.pallas_call(
        functools.partial(from_slots, count),
        out_shape=jax.ShapeDtypeStruct(received.shape, F32),
        grid_spec=pltpu.PrefetchScalarGridSpec(
            num_scalar_prefetch=1,
            grid=(slots // count,),
            in_specs=[pl.BlockSpec(received.shape, lambda q, order: (0, 0, 0, 0), pipeline_mode=pl.Buffered(1))],
            out_specs=pl.BlockSpec((count,) + received.shape[1:], lambda q, order: (q, 0, 0, 0)),
        ),
    )(q_owner, received)


def solution(mesh):
    return jax.shard_map(
        functools.partial(body, mesh.shape["pb"], mesh.shape["row"]),
        mesh=mesh,
        in_specs=(P("pb", None, "row", None), P(None, None, "pb", "row"), P(), P("pb", None)),
        out_specs=P(None, None, ("row", "pb"), None),
        check_vma=False,
    )
```

```python
import functools

import jax
import jax.numpy as jnp
from jax import lax
from jax.experimental import pallas as pl
from jax.experimental.pallas import tpu as pltpu
from jax.sharding import PartitionSpec as P

F32 = jnp.float32
BF16 = jnp.bfloat16


def from_slots(count, order, source, target):
    for i in range(count):
        target[i] = source[order[pl.program_id(0) * count + i]].astype(target.dtype)


def team_kernel(
    pb, rows, team, tile,
    order, unordered, screened, table, out,
    loaded, response, own_table, raw, weight, turned, owner_table, half, half_out, stage,
    load_got, chi_sent, chi_got, w_sent, w_got, f_sent, f_got, g_sent, g_got, h_sent, h_got, o_sent, o_got,
):
    slots = response.shape[0]
    per_pb = screened.shape[0]
    size = screened.shape[3]
    groups = pb // team
    block_rows, block_cols = response.shape[2], response.shape[3]
    own_cols = size // team
    w_rows = size // rows
    w_part = w_rows // team
    spread = rows // team
    dests = pb // team
    out_rows = out.shape[2]
    near = rows // 2

    p, r = lax.axis_index("pb"), lax.axis_index("row")
    t, group = p % team, p // team
    slot = group * rows + r

    def same(a, b):
        return jnp.logical_and(a == p, b == r)

    load = pltpu.make_async_copy(unordered, loaded, load_got)
    load.start()
    barrier = pltpu.get_barrier_semaphore()

    def greet(k, carry):
        @pl.when(k != p * rows + r)
        def _():
            pl.semaphore_signal(barrier, inc=1, device_id=(k // rows, k % rows), device_id_type=pl.DeviceIdType.MESH)
        return carry

    lax.fori_loop(0, pb * rows, greet, 0)

    for i in range(per_pb):
        @pl.when(r % per_pb == i)
        def _():
            own_table[...] = table[i : i + 1, :]

    load.wait()

    def arrange(number, carry):
        q = 0
        for i in range(1, slots):
            q = jnp.where(order[i] == number, i, q)
        response[number] = loaded[q]
        return carry

    lax.fori_loop(0, slots, arrange, 0)
    pl.semaphore_wait(barrier, pb * rows - 1)

    def send(src, dst, sent, got, at_p, at_r):
        @pl.when(same(at_p, at_r))
        def _():
            pltpu.make_async_copy(src, dst, got).start()

        @pl.when(jnp.logical_not(same(at_p, at_r)))
        def _():
            remote(src, dst, sent, got, at_p, at_r).start()

    def remote(src, dst, sent, got, at_p, at_r):
        return pltpu.make_async_remote_copy(
            src_ref=src, dst_ref=dst, send_sem=sent, recv_sem=got,
            device_id=(at_p, at_r), device_id_type=pl.DeviceIdType.MESH,
        )

    def arrived(ref, sem):
        pltpu.make_async_copy(ref, ref, sem).wait()

    def left(ref, sem, at_p, at_r):
        @pl.when(jnp.logical_not(same(at_p, at_r)))
        def _():
            pltpu.make_async_copy(ref, ref, sem).wait()

    def far_first(k):
        side = r // near
        across = (1 - side) * near + (r + k) % near
        beside = side * near + (r + 1 + k) % near
        return jnp.where(k < near, across, beside)

    holder = r // per_pb
    @pl.when(t == holder)
    def _():
        pltpu.make_async_copy(own_table, owner_table, g_got).start()
        for step in range(1, team):
            remote(own_table, owner_table, g_sent.at[step - 1], g_got, group * team + (t + step) % team, r).start()

    def w_target(block, part):
        start = pl.multiple_of(block * w_rows + part * w_part, w_part)
        return weight.at[:, pl.ds(start, w_part), :]

    def w_place(k):
        i, part = k // team, k % team
        return i, part, group * team + part, t * per_pb + i

    def w_send(k, carry):
        i, part, at_p, at_r = w_place(k)
        src = screened.at[i, :, pl.ds(pl.multiple_of(part * w_part, w_part), w_part), :]
        send(src, w_target(r, part), w_sent.at[k], w_got.at[r], at_p, at_r)
        return carry


    lax.fori_loop(0, per_pb * team, w_send, 0)

    member = r // spread

    def chi_place(k):
        at_r = far_first(k // groups)
        at_group = (group + k) % groups
        return at_group * rows + at_r, at_group * team + member, at_r

    def chi_target(from_p, from_r):
        return raw.at[
            :,
            pl.ds(pl.multiple_of(from_p * block_rows, block_rows), block_rows),
            pl.ds(pl.multiple_of((from_r % spread) * block_cols, block_cols), block_cols),
        ]

    def chi_send(k, carry):
        number, at_p, at_r = chi_place(k)
        send(response.at[number], chi_target(p, r), chi_sent.at[k], chi_got.at[p * spread + r % spread], at_p, at_r)
        return carry

    lax.fori_loop(0, slots, chi_send, 0)

    def forward(block, step):
        at_p = group * team + (t + step) % team
        ref = w_target(block, t)
        return remote(ref, ref, f_sent.at[block * team + step], f_got.at[block * team + step], at_p, r)

    def take(block):
        arrived(w_target(block, t), w_got.at[block])
        for step in range(1, team):
            forward(block, step).start()
        for step in range(1, team):
            arrived(w_target(block, (t + team - step) % team), f_got.at[block * team + step])

    def hand(block, step):
        at_p = group * team + (t + step) % team
        return remote(
            half_out.at[step - 1, block], half.at[t, block],
            h_sent.at[block * team + step], h_got.at[block * team + step], at_p, r,
        )

    def take_turn(k, carry):
        take((r + k) % rows)
        return carry

    lax.fori_loop(0, rows, take_turn, 0)
    arrived(owner_table, g_got)

    def reorder(k, carry):
        start = pl.multiple_of((k // 2) * tile, tile)
        wanted = lax.broadcasted_iota(jnp.int32, (tile, size), 0) + start
        chosen = (wanted == owner_table[...]).astype(F32).astype(BF16)
        turned[k % 2, :, pl.ds(start, tile)] = lax.dot_general(
            weight[k % 2], chosen, (((1,), (1,)), ((), ())), preferred_element_type=F32
        ).astype(BF16)
        return carry

    lax.fori_loop(0, 2 * (size // tile), reorder, 0)

    def first(block, c):
        for step in range(1, team + 1):
            part = (t + step) % team
            start = pl.multiple_of(block * w_rows + part * w_part, w_part)
            both = jnp.concatenate(
                (turned[0, pl.ds(start, w_part), :], turned[1, pl.ds(start, w_part), :]), axis=0
            )
            for cols in (slice(c * block_cols, (c + 1) * block_cols),):
                by_real = jnp.dot(both, raw[0, :, cols], preferred_element_type=F32)
                by_imag = jnp.dot(both, raw[1, :, cols], preferred_element_type=F32)
                real = (by_real[:w_part] - by_imag[w_part:]).astype(BF16)
                imag = (by_imag[:w_part] + by_real[w_part:]).astype(BF16)
                value = jnp.concatenate((real, imag), axis=0)
                if step == team:
                    half[t, block, :, cols] = value
                else:
                    half_out[step - 1, block, :, cols] = value
            if step < team and c == spread - 1:
                hand(block, step).start()

    for c in range(spread):
        def chi_wait(k, carry):
            arrived(chi_target(k, c), chi_got.at[k * spread + c])
            return carry

        def in_turn(k, carry):
            first((r + k) % rows, c)
            return carry

        lax.fori_loop(0, pb, chi_wait, 0)
        lax.fori_loop(0, rows, in_turn, 0)

    def out_send(k, m):
        at_r = far_first(k)
        send(stage.at[at_r, m], out.at[slot], o_sent.at[at_r * dests + m], o_got.at[slot], t * dests + m, at_r)

    def second(k, carry):
        block = far_first(k)
        for step in range(1, team):
            arrived(half.at[(t + team - step) % team, block], h_got.at[block * team + step])

        def columns(c, inner):
            start = pl.multiple_of(c * tile, tile)
            by_real = jnp.zeros((2 * w_part, tile), F32)
            by_imag = jnp.zeros((2 * w_part, tile), F32)
            for source in range(team):
                left_side = half[source, block]
                deep = slice(source * own_cols, (source + 1) * own_cols)
                by_real += jnp.dot(left_side, weight[0, deep, pl.ds(start, tile)], preferred_element_type=F32)
                by_imag += jnp.dot(left_side, weight[1, deep, pl.ds(start, tile)], preferred_element_type=F32)
            real = (by_real[:w_part] - by_imag[w_part:]).astype(BF16)
            imag = (by_imag[:w_part] + by_real[w_part:]).astype(BF16)
            for m in range(dests):
                lines = slice(m * out_rows, (m + 1) * out_rows)
                stage[block, m, 0, :, pl.ds(start, tile)] = real[lines]
                stage[block, m, 1, :, pl.ds(start, tile)] = imag[lines]
            return inner

        lax.fori_loop(0, size // tile, columns, 0)

        @pl.when(k > 0)
        def _():
            for m in range(dests):
                out_send(k - 1, m)
        return carry

    lax.fori_loop(0, rows, second, 0)
    for m in range(dests):
        out_send(rows - 1, m)

    def out_wait(k, carry):
        arrived(out.at[k], o_got.at[k])
        return carry

    lax.fori_loop(0, slots, out_wait, 0)

    @pl.when(t == holder)
    def _():
        for step in range(1, team):
            pltpu.make_async_copy(own_table, own_table, g_sent.at[step - 1]).wait()

    def chi_left(k, carry):
        number, at_p, at_r = chi_place(k)
        left(response.at[number], chi_sent.at[k], at_p, at_r)
        return carry

    lax.fori_loop(0, slots, chi_left, 0)

    def w_left(k, carry):
        i, part, at_p, at_r = w_place(k)
        left(w_target(r, part), w_sent.at[k], at_p, at_r)
        return carry

    lax.fori_loop(0, per_pb * team, w_left, 0)

    def blocks_left(block, carry):
        for step in range(1, team):
            forward(block, step).wait_send()
            hand(block, step).wait_send()
        for m in range(dests):
            left(stage.at[block, m], o_sent.at[block * dests + m], t * dests + m, block)
        return carry

    lax.fori_loop(0, rows, blocks_left, 0)


def body(pb, rows, screened, response, q_owner, g_index):
    slots, _, block_rows, block_cols = response.shape
    per_pb, size = screened.shape[0], screened.shape[3]
    team = pb * rows // slots
    own_cols = size // team
    w_part = size // rows // team
    out_rows = size // (pb * rows)
    dests = pb // team
    spread = rows // team
    tile = min(256, size)

    dma = pltpu.SemaphoreType.DMA
    received = pl.pallas_call(
        functools.partial(team_kernel, pb, rows, team, tile),
        out_shape=jax.ShapeDtypeStruct((slots, 2, out_rows, size), BF16),
        in_specs=[
            pl.BlockSpec(memory_space=pltpu.SMEM),
            pl.BlockSpec(memory_space=pl.ANY),
            pl.BlockSpec(memory_space=pl.ANY),
            pl.BlockSpec(memory_space=pltpu.VMEM),
        ],
        out_specs=pl.BlockSpec(memory_space=pl.ANY),
        scratch_shapes=[
            pltpu.VMEM(response.shape, BF16),
            pltpu.VMEM(response.shape, BF16),
            pltpu.VMEM((1, size), jnp.int32),
            pltpu.VMEM((2, size, own_cols), BF16),
            pltpu.VMEM((2, size, size), BF16),
            pltpu.VMEM((2, size, size), BF16),
            pltpu.VMEM((1, size), jnp.int32),
            pltpu.VMEM((team, rows, 2 * w_part, own_cols), BF16),
            pltpu.VMEM((max(team - 1, 1), rows, 2 * w_part, own_cols), BF16),
            pltpu.VMEM((rows, dests, 2, out_rows, size), BF16),
            dma(()),
            dma((slots,)),
            dma((pb * spread,)),
            dma((per_pb * team,)),
            dma((rows,)),
            dma((rows * team,)),
            dma((rows * team,)),
            dma((team,)),
            dma(()),
            dma((rows * team,)),
            dma((rows * team,)),
            dma((rows * dests,)),
            dma((slots,)),
        ],
        compiler_params=pltpu.CompilerParams(
            collective_id=0, has_side_effects=True, vmem_limit_bytes=60 * 1024 * 1024
        ),
    )(q_owner, response, screened, g_index)
    count = slots // 4
    return pl.pallas_call(
        functools.partial(from_slots, count),
        out_shape=jax.ShapeDtypeStruct(received.shape, F32),
        grid_spec=pltpu.PrefetchScalarGridSpec(
            num_scalar_prefetch=1,
            grid=(slots // count,),
            in_specs=[pl.BlockSpec(received.shape, lambda q, order: (0, 0, 0, 0), pipeline_mode=pl.Buffered(1))],
            out_specs=pl.BlockSpec((count,) + received.shape[1:], lambda q, order: (q, 0, 0, 0)),
        ),
    )(q_owner, received)


def solution(mesh):
    return jax.shard_map(
        functools.partial(body, mesh.shape["pb"], mesh.shape["row"]),
        mesh=mesh,
        in_specs=(P("pb", None, "row", None), P(None, None, "pb", "row"), P(), P("pb", None)),
        out_specs=P(None, None, ("row", "pb"), None),
        check_vma=False,
    )
```
